256 devices in a mesh: blk: 256 (over y, z, x, core).
Axes of the slice: x: 4, y: 4, z: 8, core: 2. Of those that a mesh axis runs over, the one named last changes fastest.
Arguments:
- tensor_blocks: bfloat16 [512, 32, 32, 1024], P('blk')
- block_index: int32 [512, 4], P('blk'), may hold values from 0 to 8, as said below
- starts: float32 [256, 256], P(None, 'blk'), may hold values from -6 to 6
- shifts: float32 [256], replicated, may hold values from 0.5 to 2
Outputs:
- iterate: float32 [256, 256], P(None, 'blk')
- estimate: float32 [256], P('blk')
The draws below stay inside these ranges and needn't reach their ends.
Inputs may be any that keep to these rules, and one draw needn't show every extreme that they name: `block_index`: every sorted quadruple i <= j <= k <= l of 0 to 7 is held by exactly one slot; every other slot holds 8 in all four entries and is not used. A live slot's block is unchanged when two of its axes with equal block indices are swapped.
All inputs are finite; a program needn't handle non-finite values.
Results may differ from the reference program's by a relative error of at most 0.009.
Values sent between devices are 32-bit elements; how exact they have to be, the bound alone decides.
A program may use at most 64 MiB of HBM per device.

```python
import math
import jax
import jax.numpy as jnp
import numpy as np
from jax import lax

NSIZE = 256
BS = 32
ITERS = 2
SLOTS = 512
STARTS = 256


def quadruple_table(count):
    rows_list = []
    for first in range(count):
        for second in range(first, count):
            for third in range(second, count):
                for fourth in range(third, count):
                    rows_list.append([first, second, third, fourth])
    return np.array(rows_list, dtype=np.int32)


def orderings():
    listing = []
    for first in range(4):
        for second in range(4):
            for third in range(4):
                for fourth in range(4):
                    if len(set([first, second, third, fourth])) == 4:
                        listing.append((first, second, third, fourth))
    return listing


def slot_table(key):
    count = NSIZE // BS
    quadruples = jnp.asarray(quadruple_table(count))
    order = jax.random.permutation(jax.random.fold_in(key, 7), SLOTS)
    table = jnp.full((SLOTS, 4), count, jnp.int32)
    return table.at[order[:quadruples.shape[0]]].set(quadruples)


def draw_block_index(key, part):
    return slot_table(key)


def draw_tensor_blocks(key, part):
    table = slot_table(key)
    slot_keys = jax.random.split(jax.random.fold_in(key, 11), SLOTS)
    listing = orderings()
    scale_value = float(NSIZE) ** (-1.5)

    def make_slot(item):
        slot_key, indices = item
        raw_values = jax.random.normal(slot_key, (BS, BS, BS, BS), jnp.float32)
        total = jnp.zeros((BS, BS, BS, BS), jnp.float32)
        matched = jnp.float32(0.0)
        for ordering in listing:
            moved = jnp.stack([indices[ordering[0]], indices[ordering[1]], indices[ordering[2]], indices[ordering[3]]])
            agree = jnp.all(moved == indices).astype(jnp.float32)
            total = total + agree * jnp.transpose(raw_values, ordering)
            matched = matched + agree
        block = total / matched * scale_value
        return block.reshape(BS, BS, BS * BS).astype(jnp.bfloat16)
    return lax.map(make_slot, (slot_keys, table))


def level_of(own_key, shape, shards, least, high):
    def one(dim, blocks):
        heights = jax.random.uniform(jax.random.fold_in(jax.random.fold_in(own_key, 6), dim), (blocks,), jnp.float32, least / len(shards), high / len(shards))
        return jnp.repeat(jnp.exp(heights), shape[dim] // blocks).reshape((-1,) + (1,) * (len(shape) - dim - 1))

    gain = one(*shards[0])
    for cut in shards[1:]:
        gain = gain * one(*cut)
    return gain


def bell_draw(rng, extent, spread, bound, cuts=(), kind=jnp.bfloat16):
    entries = jax.random.normal(rng, extent, jnp.float32) * spread
    if len(cuts) > 0:
        entries = level_of(rng, extent, cuts, -0.22, 0.18) * entries
    return jnp.clip(entries, min=-bound, max=bound).astype(kind)


def setup_inputs(seed: int = 0) -> dict:
    streams_of = jax.random.split(jax.random.key(seed), 5)
    return {
        "tensor_blocks": draw_tensor_blocks(jax.random.fold_in(streams_of[4], 71), 0),
        "block_index": draw_block_index(jax.random.fold_in(streams_of[4], 71), 0),
        "starts": bell_draw(streams_of[2], (NSIZE, STARTS), 1.0, 6.0, ((1, 256),), jnp.float32),
        "shifts": jnp.clip(jnp.exp(jax.random.uniform(streams_of[3], (STARTS,), jnp.float32, math.log(0.5), math.log(2.0))), 0.5, 2.0),
    }


letters = 'abcd'

def normalize(values):
    return values * lax.rsqrt(lax.optimization_barrier(jnp.mean(values * values, axis=0)) + 1e-06)

def factor_product(indices):
    product = jnp.float32(1.0)
    for other in range(1, 4):
        earlier = jnp.float32(0.0)
        for before in range(other):
            earlier = earlier + (indices[before] == indices[other]).astype(jnp.float32)
        product = product * (1.0 + earlier)
    return product

def contract_axis(tensor, pieces, position):
    others = [other for other in range(4) if other != position]
    leading = others[0]
    paired = (pieces[others[1]][:, None, :] * pieces[others[2]][None, :, :]).astype(jnp.bfloat16)
    kept = ''.join(sorted(letters[position] + letters[leading]))
    pattern = 'abcd,' + letters[others[1]] + letters[others[2]] + 'r->' + kept + 'r'
    partial_sum = jnp.einsum(pattern, tensor.astype(jnp.float32), paired.astype(jnp.float32), precision=lax.Precision.HIGHEST)
    if position < leading:
        return lax.optimization_barrier(jnp.sum(partial_sum * pieces[leading][None, :, :], axis=1))
    return lax.optimization_barrier(jnp.sum(partial_sum * pieces[leading][:, None, :], axis=0))

def apply_tensor(tensor_blocks, block_index, current):
    blocks_count = NSIZE // BS

    def one_slot(total, item):
        merged, indices = item
        tensor = merged.reshape(BS, BS, BS, BS)
        live = (indices[0] < blocks_count).astype(jnp.float32)
        safe = jnp.minimum(indices, blocks_count - 1).astype(jnp.int32)
        pieces = [lax.dynamic_slice_in_dim(current, safe[other] * BS, BS, 0) for other in range(4)]
        weight = live * 6.0 / factor_product(indices)
        for position in range(4):
            result = weight * contract_axis(tensor, pieces, position)
            start = safe[position] * BS
            total = lax.dynamic_update_slice_in_dim(total, lax.dynamic_slice_in_dim(total, start, BS, 0) + result, start, 0)
        return (total, None)
    total, unused = lax.scan(one_slot, jnp.zeros(current.shape, jnp.float32), (tensor_blocks, block_index))
    return total

def reference(tensor_blocks, block_index, starts, shifts):
    current = normalize(starts)
    previous = current
    applied = current
    for step_id in range(ITERS):
        applied = apply_tensor(tensor_blocks, block_index, current)
        previous = current
        current = normalize(applied + shifts[None, :] * current)
    estimate = lax.optimization_barrier(jnp.mean(previous * applied, axis=0)) * lax.rsqrt(lax.optimization_barrier(jnp.mean(applied * applied, axis=0)) + 1e-06)
    return (current, estimate)
```

```python
import functools

import jax
import jax.numpy as jnp
from jax import lax
from jax.experimental import pallas as pl
from jax.experimental.pallas import tpu as pltpu
from jax.sharding import Mesh
from jax.sharding import PartitionSpec as P

BLK = ("y", "z", "x", "c")
TORUS = (4, 8, 4, 2)
MESH = pl.DeviceIdType.MESH
EPS = 1e-06


def normalized(values):
    return values * lax.rsqrt(jnp.mean(values * values, axis=0, keepdims=True) + EPS)


def slot_weight(idx, blocks_count):
    weight = jnp.where(idx[0] < blocks_count, 6.0, 0.0)
    for other in range(1, 4):
        earlier = jnp.zeros(idx[0].shape, jnp.int32)
        for before in range(other):
            earlier = earlier + jnp.where(idx[before] == idx[other], 1, 0)
        share = jnp.ones(idx[0].shape, jnp.float32)
        for count in range(1, other + 1):
            share = jnp.where(earlier == count, 1.0 / (1 + count), share)
        weight = weight * share
    return weight


def kernel(
    sizes,
    torus,
    bi_ref,
    shifts_sref,
    shifts_ref,
    starts_ref,
    tensor_ref,
    out_ref,
    est_ref,
    mats,
    pair,
    cur,
    pieces,
    ybuf,
    total,
    zrows,
    ztile,
    cols,
    arrived,
    zsums,
    zpart,
    zparts,
    image,
    flipped,
    arrived2,
    zsend,
    zlast,
    send_sem,
    recv_sem,
    load_sem,
):
    slots, bs, nsize, starts = sizes
    ny, nz, nx, nc = torus
    group = ny * nx * nc
    blocks_count = nsize // bs
    piece = nsize // group
    y, z, x, c = (lax.axis_index(name) for name in BLK)
    me = (y * nx + x) * nc + c

    loads = []
    for s in range(slots):
        load = pltpu.make_async_copy(tensor_ref.at[s], mats.at[2 * s], load_sem.at[s])
        load.start()
        loads.append(load)

    plane = []
    for dy in range(ny):
        for dx in range(nx):
            for dc in range(nc):
                if dy or dx or dc:
                    py = lax.rem(y + dy, ny)
                    px = lax.rem(x + dx, nx)
                    pc = lax.rem(c + dc, nc)
                    plane.append(((py, z, px, pc), (py * nx + px) * nc + pc))
    line = []
    for dz in range(1, nz):
        pz = lax.rem(z + dz, nz)
        line.append(((y, pz, x, c), pz))

    barrier = pltpu.get_barrier_semaphore()
    for peer, _ in plane + line:
        pl.semaphore_signal(barrier, inc=1, device_id=peer, device_id_type=MESH)
    pl.semaphore_wait(barrier, len(plane) + len(line))

    def send(phase, src, dst, peer):
        pltpu.make_async_remote_copy(
            src_ref=src,
            dst_ref=dst,
            send_sem=send_sem.at[phase],
            recv_sem=recv_sem.at[phase],
            device_id=peer,
            device_id_type=MESH,
        ).start()

    def wait(sem, span):
        pltpu.make_async_copy(span, span, sem).wait()

    for peer, _ in line:
        send(0, starts_ref, zrows.at[z], peer)
    own = pltpu.make_async_copy(starts_ref, zrows.at[z], load_sem.at[slots])
    own.start()

    def flip(s):
        loads[s].wait()
        side = bs * bs
        step = min(side, 256)
        for i in range(0, side, step):
            for j in range(0, side, step):
                tile = mats[2 * s, i : i + step, j : j + step]
                mats[2 * s + 1, j : j + step, i : i + step] = tile.T

    held = lax.broadcasted_iota(jnp.int32, (starts, starts), 1)
    given = lax.broadcasted_iota(jnp.int32, (starts, starts), 0)
    hz = held % nz
    hc = (held // nz) % nc
    hx = (held // (nz * nc)) % nx
    hy = held // (nz * nc * nx)
    where_from = ((hy * nz + hz) * nx + hx) * nc + hc
    chosen = jnp.where(given == where_from, 1.0, 0.0).astype(jnp.float32)
    shifts = jnp.dot(
        jnp.broadcast_to(shifts_ref[...], (8, starts)),
        chosen,
        precision=lax.Precision.HIGHEST,
        preferred_element_type=jnp.float32,
    )[0:1, :]

    own.wait()
    wait(recv_sem.at[0], zrows.at[pl.ds(0, nz - 1)])
    ztile[...] = zrows[...].reshape(nz, nsize)
    for peer, _ in plane:
        send(1, ztile, cols.at[me], peer)
    for s in range(slots):
        flip(s)
    wait(recv_sem.at[1], cols.at[pl.ds(0, group - 1)])
    cols[me] = ztile[...]
    cur[0] = normalized(cols[...].reshape(starts, nsize).T)

    def index(s, position):
        return bi_ref[s : s + 1, position : position + 1]

    def spot(s, position):
        safe = jnp.minimum(index(s, position), blocks_count - 1)
        return jnp.broadcast_to(safe, (bs, starts))

    def contract(turn):
        for s in range(slots):
            for position in range(4):
                at = spot(s, position)
                rows = cur[turn, 0:bs, :]
                for p in range(1, blocks_count):
                    rows = jnp.where(at == p, cur[turn, p * bs : (p + 1) * bs, :], rows)
                pieces[4 * s + position] = rows

        def one(q, carry):
            s = q // 2
            m = q % 2
            side = bs * bs

            def rows(position):
                return pieces[4 * s + position]

            first, second = rows(2 - 2 * m), rows(3 - 2 * m)
            for a in range(bs):
                pair[a * bs : (a + 1) * bs, :] = (first[a : a + 1, :] * second).astype(
                    jnp.bfloat16
                )
            lead, trail = rows(2 * m), rows(2 * m + 1)
            down = jnp.zeros((bs, starts), jnp.float32)
            per = min(bs, 8)
            for t in range(0, bs, per):
                part = jnp.dot(
                    mats[q, t * bs : (t + per) * bs, :],
                    pair[...],
                    preferred_element_type=jnp.float32,
                ).reshape(per, bs, starts)
                ybuf[2 * q, t : t + per, :] = jnp.sum(part * trail[None], axis=1)
                for a in range(per):
                    down = down + part[a] * lead[t + a : t + a + 1, :]
            ybuf[2 * q + 1] = down
            return carry

        lax.fori_loop(0, 2 * slots, one, 0)
        sums = [jnp.zeros((bs, starts), jnp.float32) for _ in range(blocks_count)]
        for s in range(slots):
            weight = slot_weight([index(s, position) for position in range(4)], blocks_count)
            for position in range(4):
                part = ybuf[4 * s + position] * weight
                at = spot(s, position)
                for p in range(blocks_count):
                    sums[p] = sums[p] + jnp.where(at == p, part, 0.0)
        return sums

    sums = contract(0)
    for p in range(blocks_count):
        total[p * bs : (p + 1) * bs, :] = sums[p]
    for peer, other in plane:
        send(2, total.at[pl.ds(pl.multiple_of(other * piece, piece), piece)], arrived.at[me], peer)
    arrived[me] = total[pl.ds(pl.multiple_of(me * piece, piece), piece), :]
    wait(recv_sem.at[2], arrived.at[pl.ds(0, group - 1)])
    zpart[...] = jnp.sum(arrived[...], axis=0)
    for peer, _ in line:
        send(3, zpart, zparts.at[z], peer)
    zparts[z] = zpart[...]
    wait(recv_sem.at[3], zparts.at[pl.ds(0, nz - 1)])
    zsums[...] = jnp.sum(zparts[...], axis=0)
    for peer, _ in plane:
        send(4, zsums, image.at[me], peer)
    image[me] = zsums[...]
    wait(recv_sem.at[4], image.at[pl.ds(0, group - 1)])
    cur[1] = normalized(image[...].reshape(nsize, starts) + shifts * cur[0])

    sums = contract(1)
    for p in range(blocks_count):
        flipped[:, p * bs : (p + 1) * bs] = sums[p].T
    for peer, other in plane:
        send(5, flipped.at[pl.ds(pl.multiple_of(other * nz, nz), nz)], arrived2.at[me], peer)
    arrived2[me] = flipped[pl.ds(pl.multiple_of(me * nz, nz), nz), :]
    cols[...] = cur[1].T.reshape(group, nz, nsize)
    wait(recv_sem.at[5], arrived2.at[pl.ds(0, group - 1)])
    zsend[...] = jnp.sum(arrived2[...], axis=0).reshape(nz, 1, nsize)
    for peer, other in line:
        send(6, zsend.at[other], zlast.at[z], peer)
    zlast[z] = zsend[z]
    previous = cols[me, pl.ds(z, 1), :]
    own_shift = shifts_sref[((y * nz + z) * nx + x) * nc + c]
    wait(recv_sem.at[6], zlast.at[pl.ds(0, nz - 1)])
    mine = jnp.sum(zlast[...], axis=0)
    last = mine + own_shift * previous
    out_ref[...] = last * lax.rsqrt(jnp.mean(last * last, axis=1, keepdims=True) + EPS)
    scale = lax.rsqrt(jnp.mean(mine * mine, axis=1, keepdims=True) + EPS)
    est_ref[...] = jnp.mean(previous * mine, axis=1, keepdims=True) * scale

    spans = (zrows, cols, arrived, zparts, image, arrived2, zlast)
    for phase, span in enumerate(spans):
        wait(send_sem.at[phase], span.at[pl.ds(0, span.shape[0] - 1)])


def body(torus, tensor_blocks, block_index, starts, shifts):
    slots, bs = tensor_blocks.shape[:2]
    nsize = starts.shape[0]
    count = shifts.shape[0]
    ny, nz, nx, nc = torus
    group = ny * nx * nc
    piece = nsize // group
    side = bs * bs
    f32 = jnp.float32
    vmem, smem = pltpu.MemorySpace.VMEM, pltpu.MemorySpace.SMEM
    phases = 7
    iterate, estimate = pl.pallas_call(
        functools.partial(kernel, (slots, bs, nsize, count), torus),
        out_shape=(
            jax.ShapeDtypeStruct((1, nsize), f32),
            jax.ShapeDtypeStruct((1, 1), f32),
        ),
        in_specs=[
            pl.BlockSpec(memory_space=vmem),
            pl.BlockSpec(memory_space=smem),
            pl.BlockSpec(memory_space=vmem),
            pl.BlockSpec(memory_space=pl.ANY),
            pl.BlockSpec(memory_space=pl.ANY),
        ],
        out_specs=(pl.BlockSpec(memory_space=vmem), pl.BlockSpec(memory_space=vmem)),
        scratch_shapes=[
            pltpu.VMEM((2 * slots, side, side), jnp.bfloat16),
            pltpu.VMEM((side, count), jnp.bfloat16),
            pltpu.VMEM((2, nsize, count), f32),
            pltpu.VMEM((4 * slots, bs, count), f32),
            pltpu.VMEM((4 * slots, bs, count), f32),
            pltpu.VMEM((nsize, count), f32),
            pltpu.VMEM((nz, 1, nsize), f32),
            pltpu.VMEM((nz, nsize), f32),
            pltpu.VMEM((group, nz, nsize), f32),
            pltpu.VMEM((group, piece, count), f32),
            pltpu.VMEM((piece, count), f32),
            pltpu.VMEM((piece, count), f32),
            pltpu.VMEM((nz, piece, count), f32),
            pltpu.VMEM((group, piece, count), f32),
            pltpu.VMEM((count, nsize), f32),
            pltpu.VMEM((group, nz, nsize), f32),
            pltpu.VMEM((nz, 1, nsize), f32),
            pltpu.VMEM((nz, 1, nsize), f32),
            pltpu.SemaphoreType.DMA((phases,)),
            pltpu.SemaphoreType.DMA((phases,)),
            pltpu.SemaphoreType.DMA((slots + 1,)),
        ],
        compiler_params=pltpu.CompilerParams(collective_id=0, has_side_effects=True),
        name="power",
    )(
        block_index,
        shifts,
        shifts.reshape(1, count),
        starts.reshape(1, nsize),
        tensor_blocks.reshape(slots, side, side),
    )
    return iterate.reshape(nsize, 1), estimate.reshape(1)


def solution(mesh):
    torus = Mesh(mesh.devices.reshape(TORUS), BLK)
    in_specs = (P(BLK, None, None, None), P(BLK, None), P(None, BLK), P())
    out_specs = (P(None, BLK), P(BLK))
    return jax.shard_map(
        functools.partial(body, TORUS), mesh=torus, in_specs=in_specs, out_specs=out_specs, check_vma=False
    )
```

```python
import functools

import jax
import jax.numpy as jnp
from jax import lax
from jax.experimental import pallas as pl
from jax.experimental.pallas import tpu as pltpu
from jax.sharding import Mesh
from jax.sharding import PartitionSpec as P

BLK = ("y", "z", "x", "c")
TORUS = (4, 8, 4, 2)
MESH = pl.DeviceIdType.MESH
EPS = 1e-06


def normalized(values):
    return values * lax.rsqrt(jnp.mean(values * values, axis=0, keepdims=True) + EPS)


def slot_weight(idx, blocks_count):
    weight = jnp.where(idx[0] < blocks_count, 6.0, 0.0)
    for other in range(1, 4):
        earlier = jnp.zeros(idx[0].shape, jnp.int32)
        for before in range(other):
            earlier = earlier + jnp.where(idx[before] == idx[other], 1, 0)
        share = jnp.ones(idx[0].shape, jnp.float32)
        for count in range(1, other + 1):
            share = jnp.where(earlier == count, 1.0 / (1 + count), share)
        weight = weight * share
    return weight


def kernel(
    sizes,
    torus,
    bi_hbm,
    shifts_hbm,
    starts_ref,
    tensor_ref,
    out_ref,
    mats,
    pair,
    cur,
    pieces,
    ybuf,
    total,
    zrows,
    ztile,
    cols,
    arrived,
    zsums,
    zpart,
    zparts,
    image,
    flipped,
    arrived2,
    zsend,
    zlast,
    bi_ref,
    shifts_ref,
    send_sem,
    recv_sem,
    load_sem,
):
    slots, bs, nsize, starts = sizes
    ny, nz, nx, nc = torus
    group = ny * nx * nc
    blocks_count = nsize // bs
    piece = nsize // group
    y, z, x, c = (lax.axis_index(name) for name in BLK)
    me = (y * nx + x) * nc + c

    own = pltpu.make_async_copy(starts_ref, zrows.at[z], load_sem.at[slots])
    own.start()
    small = [
        pltpu.make_async_copy(shifts_hbm, shifts_ref, load_sem.at[slots + 1]),
        pltpu.make_async_copy(bi_hbm, bi_ref, load_sem.at[slots + 2]),
    ]
    for load in small:
        load.start()
    loads = []
    for s in range(slots):
        load = pltpu.make_async_copy(tensor_ref.at[s], mats.at[2 * s], load_sem.at[s])
        load.start()
        loads.append(load)

    plane = []
    for dy in range(ny):
        for dx in range(nx):
            for dc in range(nc):
                if dy or dx or dc:
                    py = lax.rem(y + dy, ny)
                    px = lax.rem(x + dx, nx)
                    pc = lax.rem(c + dc, nc)
                    plane.append(((py, z, px, pc), (py * nx + px) * nc + pc))
    line = []
    for dz in range(1, nz):
        pz = lax.rem(z + dz, nz)
        line.append(((y, pz, x, c), pz))

    barrier = pltpu.get_barrier_semaphore()
    for peer, _ in plane + line:
        pl.semaphore_signal(barrier, inc=1, device_id=peer, device_id_type=MESH)
    own.wait()
    pl.semaphore_wait(barrier, len(plane) + len(line))

    def send(phase, src, dst, peer):
        pltpu.make_async_remote_copy(
            src_ref=src,
            dst_ref=dst,
            send_sem=send_sem.at[phase],
            recv_sem=recv_sem.at[phase],
            device_id=peer,
            device_id_type=MESH,
        ).start()

    def wait(sem, span):
        pltpu.make_async_copy(span, span, sem).wait()

    for peer, _ in line:
        send(0, zrows.at[z], zrows.at[z], peer)

    def flip(s):
        loads[s].wait()
        side = bs * bs
        step = min(side, 256)
        for i in range(0, side, step):
            for j in range(0, side, step):
                tile = mats[2 * s, i : i + step, j : j + step]
                mats[2 * s + 1, j : j + step, i : i + step] = tile.T

    wait(recv_sem.at[0], zrows.at[pl.ds(0, nz - 1)])
    ztile[...] = zrows[...].reshape(nz, nsize)
    for peer, _ in plane:
        send(1, ztile, cols.at[me], peer)
    for load in small:
        load.wait()
    column = ((y * nz + z) * nx + x) * nc + c
    lane = lax.broadcasted_iota(jnp.int32, (1, starts), 1)
    own_shift = jnp.sum(jnp.where(lane == column, shifts_ref[...], 0.0), axis=1, keepdims=True)
    held = lax.broadcasted_iota(jnp.int32, (starts, starts), 1)
    given = lax.broadcasted_iota(jnp.int32, (starts, starts), 0)
    hz = held % nz
    hc = (held // nz) % nc
    hx = (held // (nz * nc)) % nx
    hy = held // (nz * nc * nx)
    where_from = ((hy * nz + hz) * nx + hx) * nc + hc
    chosen = jnp.where(given == where_from, 1.0, 0.0).astype(jnp.float32)
    shifts = jnp.dot(
        jnp.broadcast_to(shifts_ref[...], (8, starts)),
        chosen,
        precision=lax.Precision.HIGHEST,
        preferred_element_type=jnp.float32,
    )[0:1, :]

    for s in range(slots):
        flip(s)
    wait(recv_sem.at[1], cols.at[pl.ds(0, group - 1)])
    cols[me] = ztile[...]
    cur[0] = normalized(cols[...].reshape(starts, nsize).T)

    def index(s, position):
        return bi_ref[s : s + 1, position : position + 1]

    def spot(s, position):
        safe = jnp.minimum(index(s, position), blocks_count - 1)
        return jnp.broadcast_to(safe, (bs, starts))

    def contract(turn):
        for s in range(slots):
            for position in range(4):
                at = spot(s, position)
                rows = cur[turn, 0:bs, :]
                for p in range(1, blocks_count):
                    rows = jnp.where(at == p, cur[turn, p * bs : (p + 1) * bs, :], rows)
                pieces[4 * s + position] = rows

        def one(q, carry):
            s = q // 2
            m = q % 2
            side = bs * bs

            def rows(position):
                return pieces[4 * s + position]

            first, second = rows(2 - 2 * m), rows(3 - 2 * m)
            for a in range(bs):
                pair[a * bs : (a + 1) * bs, :] = (first[a : a + 1, :] * second).astype(
                    jnp.bfloat16
                )
            lead, trail = rows(2 * m), rows(2 * m + 1)
            down = jnp.zeros((bs, starts), jnp.float32)
            per = min(bs, 8)
            for t in range(0, bs, per):
                part = jnp.dot(
                    mats[q, t * bs : (t + per) * bs, :],
                    pair[...],
                    preferred_element_type=jnp.float32,
                ).reshape(per, bs, starts)
                ybuf[2 * q, t : t + per, :] = jnp.sum(part * trail[None], axis=1)
                for a in range(per):
                    down = down + part[a] * lead[t + a : t + a + 1, :]
            ybuf[2 * q + 1] = down
            return carry

        lax.fori_loop(0, 2 * slots, one, 0, unroll=True)
        sums = [jnp.zeros((bs, starts), jnp.float32) for _ in range(blocks_count)]
        for s in range(slots):
            weight = slot_weight([index(s, position) for position in range(4)], blocks_count)
            for position in range(4):
                part = ybuf[4 * s + position] * weight
                at = spot(s, position)
                for p in range(blocks_count):
                    sums[p] = sums[p] + jnp.where(at == p, part, 0.0)
        return sums

    sums = contract(0)
    for p in range(blocks_count):
        total[p * bs : (p + 1) * bs, :] = sums[p]
    for peer, other in plane:
        send(2, total.at[pl.ds(pl.multiple_of(other * piece, piece), piece)], arrived.at[me], peer)
    arrived[me] = total[pl.ds(pl.multiple_of(me * piece, piece), piece), :]
    wait(recv_sem.at[2], arrived.at[pl.ds(0, group - 1)])
    zpart[...] = jnp.sum(arrived[...], axis=0)
    for peer, _ in line:
        send(3, zpart, zparts.at[z], peer)
    zparts[z] = zpart[...]
    wait(recv_sem.at[3], zparts.at[pl.ds(0, nz - 1)])
    zsums[...] = jnp.sum(zparts[...], axis=0)
    for peer, _ in plane:
        send(4, zsums, image.at[me], peer)
    image[me] = zsums[...]
    wait(recv_sem.at[4], image.at[pl.ds(0, group - 1)])
    cur[1] = normalized(image[...].reshape(nsize, starts) + shifts * cur[0])

    sums = contract(1)
    for p in range(blocks_count):
        flipped[:, p * bs : (p + 1) * bs] = sums[p].T
    for peer, other in plane:
        send(5, flipped.at[pl.ds(pl.multiple_of(other * nz, nz), nz)], arrived2.at[me], peer)
    arrived2[me] = flipped[pl.ds(pl.multiple_of(me * nz, nz), nz), :]
    cols[...] = cur[1].T.reshape(group, nz, nsize)
    wait(recv_sem.at[5], arrived2.at[pl.ds(0, group - 1)])
    zsend[...] = jnp.sum(arrived2[...], axis=0).reshape(nz, 1, nsize)
    for peer, other in line:
        send(6, zsend.at[other], zlast.at[z], peer)
    zlast[z] = zsend[z]
    previous = cols[me, pl.ds(z, 1), :]
    wait(recv_sem.at[6], zlast.at[pl.ds(0, nz - 1)])
    mine = jnp.sum(zlast[...], axis=0)
    last = mine + own_shift * previous
    out_ref[0:1, :] = last * lax.rsqrt(jnp.mean(last * last, axis=1, keepdims=True) + EPS)
    scale = lax.rsqrt(jnp.mean(mine * mine, axis=1, keepdims=True) + EPS)
    out_ref[1:2, :] = previous * mine * (scale / nsize)

    spans = (zrows, cols, arrived, zparts, image, arrived2, zlast)
    for phase, span in enumerate(spans):
        wait(send_sem.at[phase], span.at[pl.ds(0, span.shape[0] - 1)])


def tail(rows_ref, out_ref, est_ref):
    out_ref[...] = rows_ref[0:1, :]
    est_ref[...] = jnp.sum(rows_ref[1:2, :], axis=1, keepdims=True)


def body(torus, tensor_blocks, block_index, starts, shifts):
    slots, bs = tensor_blocks.shape[:2]
    nsize = starts.shape[0]
    count = shifts.shape[0]
    ny, nz, nx, nc = torus
    group = ny * nx * nc
    piece = nsize // group
    side = bs * bs
    f32 = jnp.float32
    vmem = pltpu.MemorySpace.VMEM
    phases = 7
    (rows,) = pl.pallas_call(
        functools.partial(kernel, (slots, bs, nsize, count), torus),
        out_shape=(
            jax.ShapeDtypeStruct((2, nsize), f32),
        ),
        in_specs=[
            pl.BlockSpec(memory_space=pl.ANY),
            pl.BlockSpec(memory_space=pl.ANY),
            pl.BlockSpec(memory_space=pl.ANY),
            pl.BlockSpec(memory_space=pl.ANY),
        ],
        out_specs=(pl.BlockSpec(memory_space=vmem),),
        scratch_shapes=[
            pltpu.VMEM((2 * slots, side, side), jnp.bfloat16),
            pltpu.VMEM((side, count), jnp.bfloat16),
            pltpu.VMEM((2, nsize, count), f32),
            pltpu.VMEM((4 * slots, bs, count), f32),
            pltpu.VMEM((4 * slots, bs, count), f32),
            pltpu.VMEM((nsize, count), f32),
            pltpu.VMEM((nz, 1, nsize), f32),
            pltpu.VMEM((nz, nsize), f32),
            pltpu.VMEM((group, nz, nsize), f32),
            pltpu.VMEM((group, piece, count), f32),
            pltpu.VMEM((piece, count), f32),
            pltpu.VMEM((piece, count), f32),
            pltpu.VMEM((nz, piece, count), f32),
            pltpu.VMEM((group, piece, count), f32),
            pltpu.VMEM((count, nsize), f32),
            pltpu.VMEM((group, nz, nsize), f32),
            pltpu.VMEM((nz, 1, nsize), f32),
            pltpu.VMEM((nz, 1, nsize), f32),
            pltpu.VMEM(block_index.shape, jnp.int32),
            pltpu.VMEM((1, count), f32),
            pltpu.SemaphoreType.DMA((phases,)),
            pltpu.SemaphoreType.DMA((phases,)),
            pltpu.SemaphoreType.DMA((slots + 3,)),
        ],
        compiler_params=pltpu.CompilerParams(collective_id=0, has_side_effects=True),
        name="power",
    )(
        block_index,
        shifts.reshape(1, count),
        starts.reshape(1, nsize),
        tensor_blocks.reshape(slots, side, side),
    )
    iterate, estimate = pl.pallas_call(
        tail,
        out_shape=(
            jax.ShapeDtypeStruct((1, nsize), f32),
            jax.ShapeDtypeStruct((1, 1), f32),
        ),
        name="tail",
    )(rows)
    return iterate.reshape(nsize, 1), estimate.reshape(1)


def solution(mesh):
    torus = Mesh(mesh.devices.reshape(TORUS), BLK)
    in_specs = (P(BLK, None, None, None), P(BLK, None), P(None, BLK), P())
    out_specs = (P(None, BLK), P(BLK))
    return jax.shard_map(
        functools.partial(body, TORUS), mesh=torus, in_specs=in_specs, out_specs=out_specs, check_vma=False
    )
```

```python
import functools

import jax
import jax.numpy as jnp
from jax import lax
from jax.experimental import pallas as pl
from jax.experimental.pallas import tpu as pltpu
from jax.sharding import Mesh
from jax.sharding import PartitionSpec as P

BLK = ("y", "z", "x", "c")
TORUS = (4, 8, 4, 2)
MESH = pl.DeviceIdType.MESH
EPS = 1e-06


def normalized(values):
    return values * lax.rsqrt(jnp.mean(values * values, axis=0, keepdims=True) + EPS)


def slot_weight(idx, blocks_count):
    weight = jnp.where(idx[0] < blocks_count, 6.0, 0.0)
    for other in range(1, 4):
        earlier = jnp.zeros(idx[0].shape, jnp.int32)
        for before in range(other):
            earlier = earlier + jnp.where(idx[before] == idx[other], 1, 0)
        share = jnp.ones(idx[0].shape, jnp.float32)
        for count in range(1, other + 1):
            share = jnp.where(earlier == count, 1.0 / (1 + count), share)
        weight = weight * share
    return weight


def kernel(
    sizes,
    torus,
    bi_hbm,
    shifts_hbm,
    starts_ref,
    tensor_ref,
    out_ref,
    mats,
    pair,
    cur,
    pieces,
    ybuf,
    total,
    zrows,
    ztile,
    cols,
    arrived,
    zsums,
    zpart,
    zparts,
    image,
    flipped,
    arrived2,
    zsend,
    zlast,
    bi_ref,
    shifts_ref,
    send_sem,
    recv_sem,
    load_sem,
):
    slots, bs, nsize, starts = sizes
    ny, nz, nx, nc = torus
    group = ny * nx * nc
    blocks_count = nsize // bs
    piece = nsize // group
    y, z, x, c = (lax.axis_index(name) for name in BLK)
    me = (y * nx + x) * nc + c

    own = pltpu.make_async_copy(starts_ref, zrows.at[z], load_sem.at[slots])
    own.start()
    small = [
        pltpu.make_async_copy(shifts_hbm, shifts_ref, load_sem.at[slots + 1]),
        pltpu.make_async_copy(bi_hbm, bi_ref, load_sem.at[slots + 2]),
    ]
    for load in small:
        load.start()
    loads = []
    for s in range(slots):
        load = pltpu.make_async_copy(tensor_ref.at[s], mats.at[2 * s], load_sem.at[s])
        load.start()
        loads.append(load)

    def hops(step, size):
        return min(step, size - step)

    steps = [(dy, dx, dc) for dy in range(ny) for dx in range(nx) for dc in range(nc)][1:]
    steps.sort(key=lambda d: -(hops(d[0], ny) + hops(d[1], nx)))
    plane = []
    for dy, dx, dc in steps:
        py = lax.rem(y + dy, ny)
        px = lax.rem(x + dx, nx)
        pc = lax.rem(c + dc, nc)
        plane.append(((py, z, px, pc), (py * nx + px) * nc + pc))
    line = []
    for dz in sorted(range(1, nz), key=lambda d: -hops(d, nz)):
        pz = lax.rem(z + dz, nz)
        line.append(((y, pz, x, c), pz))

    barrier = pltpu.get_barrier_semaphore()
    for peer, _ in plane + line:
        pl.semaphore_signal(barrier, inc=1, device_id=peer, device_id_type=MESH)
    own.wait()
    pl.semaphore_wait(barrier, len(plane) + len(line))

    def send(phase, src, dst, peer):
        pltpu.make_async_remote_copy(
            src_ref=src,
            dst_ref=dst,
            send_sem=send_sem.at[phase],
            recv_sem=recv_sem.at[phase],
            device_id=peer,
            device_id_type=MESH,
        ).start()

    def wait(sem, span):
        pltpu.make_async_copy(span, span, sem).wait()

    for peer, _ in line:
        send(0, zrows.at[z], zrows.at[z], peer)

    def flip(s):
        loads[s].wait()
        side = bs * bs
        step = min(side, 256)
        for i in range(0, side, step):
            for j in range(0, side, step):
                tile = mats[2 * s, i : i + step, j : j + step]
                mats[2 * s + 1, j : j + step, i : i + step] = tile.T

    wait(recv_sem.at[0], zrows.at[pl.ds(0, nz - 1)])
    ztile[...] = zrows[...].reshape(nz, nsize)
    for peer, _ in plane:
        send(1, ztile, cols.at[me], peer)
    for load in small:
        load.wait()
    column = ((y * nz + z) * nx + x) * nc + c
    lane = lax.broadcasted_iota(jnp.int32, (1, starts), 1)
    own_shift = jnp.sum(jnp.where(lane == column, shifts_ref[...], 0.0), axis=1, keepdims=True)
    held = lax.broadcasted_iota(jnp.int32, (starts, starts), 1)
    given = lax.broadcasted_iota(jnp.int32, (starts, starts), 0)
    hz = held % nz
    hc = (held // nz) % nc
    hx = (held // (nz * nc)) % nx
    hy = held // (nz * nc * nx)
    where_from = ((hy * nz + hz) * nx + hx) * nc + hc
    chosen = jnp.where(given == where_from, 1.0, 0.0).astype(jnp.float32)
    shifts = jnp.dot(
        jnp.broadcast_to(shifts_ref[...], (8, starts)),
        chosen,
        precision=lax.Precision.HIGHEST,
        preferred_element_type=jnp.float32,
    )[0:1, :]

    for s in range(slots):
        flip(s)
    wait(recv_sem.at[1], cols.at[pl.ds(0, group - 1)])
    cols[me] = ztile[...]
    cur[0] = normalized(cols[...].reshape(starts, nsize).T)

    def index(s, position):
        return bi_ref[s : s + 1, position : position + 1]

    def spot(s, position):
        safe = jnp.minimum(index(s, position), blocks_count - 1)
        return jnp.broadcast_to(safe, (bs, starts))

    def contract(turn):
        for s in range(slots):
            for position in range(4):
                at = spot(s, position)
                rows = cur[turn, 0:bs, :]
                for p in range(1, blocks_count):
                    rows = jnp.where(at == p, cur[turn, p * bs : (p + 1) * bs, :], rows)
                pieces[4 * s + position] = rows

        def one(q, carry):
            s = q // 2
            m = q % 2
            side = bs * bs

            def rows(position):
                return pieces[4 * s + position]

            first, second = rows(2 - 2 * m), rows(3 - 2 * m)
            for a in range(bs):
                pair[a * bs : (a + 1) * bs, :] = (first[a : a + 1, :] * second).astype(
                    jnp.bfloat16
                )
            lead, trail = rows(2 * m), rows(2 * m + 1)
            down = jnp.zeros((bs, starts), jnp.float32)
            per = min(bs, 8)
            for t in range(0, bs, per):
                part = jnp.dot(
                    mats[q, t * bs : (t + per) * bs, :],
                    pair[...],
                    preferred_element_type=jnp.float32,
                ).reshape(per, bs, starts)
                ybuf[2 * q, t : t + per, :] = jnp.sum(part * trail[None], axis=1)
                for a in range(per):
                    down = down + part[a] * lead[t + a : t + a + 1, :]
            ybuf[2 * q + 1] = down
            return carry

        lax.fori_loop(0, 2 * slots, one, 0, unroll=True)
        sums = [jnp.zeros((bs, starts), jnp.float32) for _ in range(blocks_count)]
        for s in range(slots):
            weight = slot_weight([index(s, position) for position in range(4)], blocks_count)
            for position in range(4):
                part = ybuf[4 * s + position] * weight
                at = spot(s, position)
                for p in range(blocks_count):
                    sums[p] = sums[p] + jnp.where(at == p, part, 0.0)
        return sums

    sums = contract(0)
    for p in range(blocks_count):
        total[p * bs : (p + 1) * bs, :] = sums[p]
    for peer, other in plane:
        send(2, total.at[pl.ds(pl.multiple_of(other * piece, piece), piece)], arrived.at[me], peer)
    arrived[me] = total[pl.ds(pl.multiple_of(me * piece, piece), piece), :]
    wait(recv_sem.at[2], arrived.at[pl.ds(0, group - 1)])
    zpart[...] = jnp.sum(arrived[...], axis=0)
    for peer, _ in line:
        send(3, zpart, zparts.at[z], peer)
    zparts[z] = zpart[...]
    wait(recv_sem.at[3], zparts.at[pl.ds(0, nz - 1)])
    zsums[...] = jnp.sum(zparts[...], axis=0)
    for peer, _ in plane:
        send(4, zsums, image.at[me], peer)
    image[me] = zsums[...]
    wait(recv_sem.at[4], image.at[pl.ds(0, group - 1)])
    cur[1] = normalized(image[...].reshape(nsize, starts) + shifts * cur[0])

    sums = contract(1)
    for p in range(blocks_count):
        flipped[:, p * bs : (p + 1) * bs] = sums[p].T
    for peer, other in plane:
        send(5, flipped.at[pl.ds(pl.multiple_of(other * nz, nz), nz)], arrived2.at[me], peer)
    arrived2[me] = flipped[pl.ds(pl.multiple_of(me * nz, nz), nz), :]
    cols[...] = cur[1].T.reshape(group, nz, nsize)
    wait(recv_sem.at[5], arrived2.at[pl.ds(0, group - 1)])
    zsend[...] = jnp.sum(arrived2[...], axis=0).reshape(nz, 1, nsize)
    for peer, other in line:
        send(6, zsend.at[other], zlast.at[z], peer)
    zlast[z] = zsend[z]
    previous = cols[me, pl.ds(z, 1), :]
    wait(recv_sem.at[6], zlast.at[pl.ds(0, nz - 1)])
    mine = jnp.sum(zlast[...], axis=0)
    last = mine + own_shift * previous
    out_ref[0:1, :] = last * lax.rsqrt(jnp.mean(last * last, axis=1, keepdims=True) + EPS)
    scale = lax.rsqrt(jnp.mean(mine * mine, axis=1, keepdims=True) + EPS)
    out_ref[1:2, :] = previous * mine * (scale / nsize)

    spans = (zrows, cols, arrived, zparts, image, arrived2, zlast)
    for phase, span in enumerate(spans):
        wait(send_sem.at[phase], span.at[pl.ds(0, span.shape[0] - 1)])


def tail(rows_ref, out_ref, est_ref):
    out_ref[...] = rows_ref[0:1, :]
    est_ref[...] = jnp.sum(rows_ref[1:2, :], axis=1, keepdims=True)


def body(torus, tensor_blocks, block_index, starts, shifts):
    slots, bs = tensor_blocks.shape[:2]
    nsize = starts.shape[0]
    count = shifts.shape[0]
    ny, nz, nx, nc = torus
    group = ny * nx * nc
    piece = nsize // group
    side = bs * bs
    f32 = jnp.float32
    vmem = pltpu.MemorySpace.VMEM
    phases = 7
    (rows,) = pl.pallas_call(
        functools.partial(kernel, (slots, bs, nsize, count), torus),
        out_shape=(
            jax.ShapeDtypeStruct((2, nsize), f32),
        ),
        in_specs=[
            pl.BlockSpec(memory_space=pl.ANY),
            pl.BlockSpec(memory_space=pl.ANY),
            pl.BlockSpec(memory_space=pl.ANY),
            pl.BlockSpec(memory_space=pl.ANY),
        ],
        out_specs=(pl.BlockSpec(memory_space=vmem),),
        scratch_shapes=[
            pltpu.VMEM((2 * slots, side, side), jnp.bfloat16),
            pltpu.VMEM((side, count), jnp.bfloat16),
            pltpu.VMEM((2, nsize, count), f32),
            pltpu.VMEM((4 * slots, bs, count), f32),
            pltpu.VMEM((4 * slots, bs, count), f32),
            pltpu.VMEM((nsize, count), f32),
            pltpu.VMEM((nz, 1, nsize), f32),
            pltpu.VMEM((nz, nsize), f32),
            pltpu.VMEM((group, nz, nsize), f32),
            pltpu.VMEM((group, piece, count), f32),
            pltpu.VMEM((piece, count), f32),
            pltpu.VMEM((piece, count), f32),
            pltpu.VMEM((nz, piece, count), f32),
            pltpu.VMEM((group, piece, count), f32),
            pltpu.VMEM((count, nsize), f32),
            pltpu.VMEM((group, nz, nsize), f32),
            pltpu.VMEM((nz, 1, nsize), f32),
            pltpu.VMEM((nz, 1, nsize), f32),
            pltpu.VMEM(block_index.shape, jnp.int32),
            pltpu.VMEM((1, count), f32),
            pltpu.SemaphoreType.DMA((phases,)),
            pltpu.SemaphoreType.DMA((phases,)),
            pltpu.SemaphoreType.DMA((slots + 3,)),
        ],
        compiler_params=pltpu.CompilerParams(collective_id=0, has_side_effects=True),
        name="power",
    )(
        block_index,
        shifts.reshape(1, count),
        starts.reshape(1, nsize),
        tensor_blocks.reshape(slots, side, side),
    )
    iterate, estimate = pl.pallas_call(
        tail,
        out_shape=(
            jax.ShapeDtypeStruct((1, nsize), f32),
            jax.ShapeDtypeStruct((1, 1), f32),
        ),
        name="tail",
    )(rows)
    return iterate.reshape(nsize, 1), estimate.reshape(1)


def solution(mesh):
    torus = Mesh(mesh.devices.reshape(TORUS), BLK)
    in_specs = (P(BLK, None, None, None), P(BLK, None), P(None, BLK), P())
    out_specs = (P(None, BLK), P(BLK))
    return jax.shard_map(
        functools.partial(body, TORUS), mesh=torus, in_specs=in_specs, out_specs=out_specs, check_vma=False
    )
```

```python
import functools

import jax
import jax.numpy as jnp
from jax import lax
from jax.experimental import pallas as pl
from jax.experimental.pallas import tpu as pltpu
from jax.sharding import Mesh
from jax.sharding import PartitionSpec as P

BLK = ("y", "z", "x", "c")
TORUS = (4, 8, 4, 2)
MESH = pl.DeviceIdType.MESH
EPS = 1e-06
NEAR = 2


def chip_steps(ny, nx):
    def hops(step):
        return sum(min(s, n - s) for s, n in zip(step, (ny, nx)))

    steps = [(dy, dx) for dy in range(ny) for dx in range(nx)][1:]
    steps.sort(key=lambda step: -hops(step))
    return [d for d in steps if hops(d) > NEAR], [d for d in steps if hops(d) <= NEAR]


def normalized(values):
    return values * lax.rsqrt(jnp.mean(values * values, axis=0, keepdims=True) + EPS)


def slot_weight(idx, blocks_count):
    weight = jnp.where(idx[0] < blocks_count, 6.0, 0.0)
    for other in range(1, 4):
        earlier = jnp.zeros(idx[0].shape, jnp.int32)
        for before in range(other):
            earlier = earlier + jnp.where(idx[before] == idx[other], 1, 0)
        share = jnp.ones(idx[0].shape, jnp.float32)
        for count in range(1, other + 1):
            share = jnp.where(earlier == count, 1.0 / (1 + count), share)
        weight = weight * share
    return weight


def kernel(
    sizes,
    torus,
    bi_hbm,
    shifts_hbm,
    starts_ref,
    tensor_ref,
    out_ref,
    mats,
    pair,
    cur,
    pieces,
    ybuf,
    total,
    zrows,
    ztile,
    cols,
    handed,
    merged,
    arrived,
    zsums,
    zpart,
    zparts,
    image,
    flipped,
    handed2,
    merged2,
    arrived2,
    zsend,
    zlast,
    bi_ref,
    shifts_ref,
    send_sem,
    recv_sem,
    load_sem,
):
    slots, bs, nsize, starts = sizes
    ny, nz, nx, nc = torus
    group = ny * nx * nc
    blocks_count = nsize // bs
    piece = nsize // group
    y, z, x, c = (lax.axis_index(name) for name in BLK)
    me = (y * nx + x) * nc + c

    def at(dy, dx, core):
        py = lax.rem(y + dy, ny)
        px = lax.rem(x + dx, nx)
        return (py, z, px, core), (py * nx + px) * nc + core

    far_steps, near_steps = chip_steps(ny, nx)
    other = 1 - c
    partner, partner_at = at(0, 0, other)
    far = [at(dy, dx, core) for dy, dx in far_steps for core in (c, other)]
    near = [at(dy, dx, c) for dy, dx in near_steps]
    near_other = [at(dy, dx, other) for dy, dx in near_steps]
    plane = far + [peer for pair in zip(near, near_other) for peer in pair]
    plane.append((partner, partner_at))
    line = []
    for dz in sorted(range(1, nz), key=lambda d: -min(d, nz - d)):
        pz = lax.rem(z + dz, nz)
        line.append(((y, pz, x, c), pz))
    everyone = [peer for peer, _ in line + plane]

    barrier = pltpu.get_barrier_semaphore()
    for peer in everyone:
        pl.semaphore_signal(barrier, inc=1, device_id=peer, device_id_type=MESH)
    own = pltpu.make_async_copy(starts_ref, zrows.at[z], load_sem.at[slots])
    own.start()
    small = [
        pltpu.make_async_copy(shifts_hbm, shifts_ref, load_sem.at[slots + 1]),
        pltpu.make_async_copy(bi_hbm, bi_ref, load_sem.at[slots + 2]),
    ]
    for load in small:
        load.start()
    loads = []
    for s in range(slots):
        load = pltpu.make_async_copy(tensor_ref.at[s], mats.at[2 * s], load_sem.at[s])
        load.start()
        loads.append(load)

    own.wait()
    pl.semaphore_wait(barrier, len(everyone))

    def send(phase, src, dst, peer):
        pltpu.make_async_remote_copy(
            src_ref=src,
            dst_ref=dst,
            send_sem=send_sem.at[phase],
            recv_sem=recv_sem.at[phase],
            device_id=peer,
            device_id_type=MESH,
        ).start()

    def wait(sem, span):
        pltpu.make_async_copy(span, span, sem).wait()

    def spread(phase, source, held):
        for peer, _ in plane:
            send(phase, source, held.at[me], peer)

    def spread_done(phase, source, held):
        held[me] = source[...]
        wait(recv_sem.at[phase], held.at[pl.ds(0, group - 1)])

    def collect(phase, source, handed, merged, got):
        rows = got.shape[1]

        def piece_of(place):
            return pl.ds(pl.multiple_of(place * rows, rows), rows)

        for i, (peer, place) in enumerate(far):
            send(phase + 1, source.at[piece_of(place)], got.at[len(near) + i], peer)
        for i, (_, place) in enumerate(near_other):
            send(phase, source.at[piece_of(place)], handed.at[i], partner)
        send(phase, source.at[piece_of(partner_at)], handed.at[len(near)], partner)
        wait(recv_sem.at[phase], handed)
        for i, (peer, place) in enumerate(near):
            merged[i] = source[piece_of(place), :] + handed[i]
            send(phase + 1, merged.at[i], got.at[i], peer)
        return source[piece_of(me), :] + handed[len(near)]

    for peer, _ in line:
        send(0, zrows.at[z], zrows.at[z], peer)

    def flip(s):
        loads[s].wait()
        side = bs * bs
        step = min(side, 256)
        for i in range(0, side, step):
            for j in range(0, side, step):
                tile = mats[2 * s, i : i + step, j : j + step]
                mats[2 * s + 1, j : j + step, i : i + step] = tile.T

    wait(recv_sem.at[0], zrows.at[pl.ds(0, nz - 1)])
    ztile[...] = zrows[...].reshape(nz, nsize)
    spread(1, ztile, cols)
    for load in small:
        load.wait()
    column = ((y * nz + z) * nx + x) * nc + c
    lane = lax.broadcasted_iota(jnp.int32, (1, starts), 1)
    own_shift = jnp.sum(jnp.where(lane == column, shifts_ref[...], 0.0), axis=1, keepdims=True)
    held = lax.broadcasted_iota(jnp.int32, (starts, starts), 1)
    given = lax.broadcasted_iota(jnp.int32, (starts, starts), 0)
    hz = held % nz
    hc = (held // nz) % nc
    hx = (held // (nz * nc)) % nx
    hy = held // (nz * nc * nx)
    where_from = ((hy * nz + hz) * nx + hx) * nc + hc
    chosen = jnp.where(given == where_from, 1.0, 0.0).astype(jnp.float32)
    shifts = jnp.dot(
        jnp.broadcast_to(shifts_ref[...], (8, starts)),
        chosen,
        precision=lax.Precision.HIGHEST,
        preferred_element_type=jnp.float32,
    )[0:1, :]

    for s in range(slots):
        flip(s)
    spread_done(1, ztile, cols)
    cur[0] = normalized(cols[...].reshape(starts, nsize).T)

    def index(s, position):
        return bi_ref[s : s + 1, position : position + 1]

    def spot(s, position):
        safe = jnp.minimum(index(s, position), blocks_count - 1)
        return jnp.broadcast_to(safe, (bs, starts))

    def contract(turn):
        for s in range(slots):
            for position in range(4):
                at = spot(s, position)
                rows = cur[turn, 0:bs, :]
                for p in range(1, blocks_count):
                    rows = jnp.where(at == p, cur[turn, p * bs : (p + 1) * bs, :], rows)
                pieces[4 * s + position] = rows

        def one(q, carry):
            s = q // 2
            m = q % 2
            side = bs * bs

            def rows(position):
                return pieces[4 * s + position]

            first, second = rows(2 - 2 * m), rows(3 - 2 * m)
            for a in range(bs):
                pair[a * bs : (a + 1) * bs, :] = (first[a : a + 1, :] * second).astype(
                    jnp.bfloat16
                )
            lead, trail = rows(2 * m), rows(2 * m + 1)
            down = jnp.zeros((bs, starts), jnp.float32)
            per = min(bs, 8)
            for t in range(0, bs, per):
                part = jnp.dot(
                    mats[q, t * bs : (t + per) * bs, :],
                    pair[...],
                    preferred_element_type=jnp.float32,
                ).reshape(per, bs, starts)
                ybuf[2 * q, t : t + per, :] = jnp.sum(part * trail[None], axis=1)
                for a in range(per):
                    down = down + part[a] * lead[t + a : t + a + 1, :]
            ybuf[2 * q + 1] = down
            return carry

        lax.fori_loop(0, 2 * slots, one, 0, unroll=True)
        sums = [jnp.zeros((bs, starts), jnp.float32) for _ in range(blocks_count)]
        for s in range(slots):
            weight = slot_weight([index(s, position) for position in range(4)], blocks_count)
            for position in range(4):
                part = ybuf[4 * s + position] * weight
                at = spot(s, position)
                for p in range(blocks_count):
                    sums[p] = sums[p] + jnp.where(at == p, part, 0.0)
        return sums

    sums = contract(0)
    for p in range(blocks_count):
        total[p * bs : (p + 1) * bs, :] = sums[p]
    own_piece = collect(4, total, handed, merged, arrived)
    wait(recv_sem.at[5], arrived)
    zpart[...] = own_piece + jnp.sum(arrived[...], axis=0)
    for peer, _ in line:
        send(6, zpart, zparts.at[z], peer)
    zparts[z] = zpart[...]
    wait(recv_sem.at[6], zparts.at[pl.ds(0, nz - 1)])
    zsums[...] = jnp.sum(zparts[...], axis=0)
    spread(7, zsums, image)
    spread_done(7, zsums, image)
    cur[1] = normalized(image[...].reshape(nsize, starts) + shifts * cur[0])

    sums = contract(1)
    for p in range(blocks_count):
        flipped[:, p * bs : (p + 1) * bs] = sums[p].T
    own_piece = collect(10, flipped, handed2, merged2, arrived2)
    cols[...] = cur[1].T.reshape(group, nz, nsize)
    wait(recv_sem.at[11], arrived2)
    zsend[...] = (own_piece + jnp.sum(arrived2[...], axis=0)).reshape(nz, 1, nsize)
    for peer, place in line:
        send(12, zsend.at[place], zlast.at[z], peer)
    zlast[z] = zsend[z]
    previous = cols[me, pl.ds(z, 1), :]
    wait(recv_sem.at[12], zlast.at[pl.ds(0, nz - 1)])
    mine = jnp.sum(zlast[...], axis=0)
    last = mine + own_shift * previous
    out_ref[0:1, :] = last * lax.rsqrt(jnp.mean(last * last, axis=1, keepdims=True) + EPS)
    scale = lax.rsqrt(jnp.mean(mine * mine, axis=1, keepdims=True) + EPS)
    out_ref[1:2, :] = previous * mine * (scale / nsize)

    sent = [(0, zrows, nz - 1), (6, zparts, nz - 1), (12, zlast, nz - 1)]
    for phase, span in ((1, cols), (7, image)):
        sent.append((phase, span, group - 1))
    for phase, span, span2 in ((4, handed, arrived), (10, handed2, arrived2)):
        sent += [(phase, span, len(near) + 1), (phase + 1, span2, len(near) + len(far))]
    for phase, span, count in sent:
        if count:
            wait(send_sem.at[phase], span.at[pl.ds(0, count)])


def tail(rows_ref, out_ref, est_ref):
    out_ref[...] = rows_ref[0:1, :]
    est_ref[...] = jnp.sum(rows_ref[1:2, :], axis=1, keepdims=True)


def body(torus, tensor_blocks, block_index, starts, shifts):
    slots, bs = tensor_blocks.shape[:2]
    nsize = starts.shape[0]
    count = shifts.shape[0]
    ny, nz, nx, nc = torus
    group = ny * nx * nc
    piece = nsize // group
    side = bs * bs
    f32 = jnp.float32
    vmem = pltpu.MemorySpace.VMEM
    far, near = (len(part) for part in chip_steps(ny, nx))
    far = far * nc
    phases = 13
    (rows,) = pl.pallas_call(
        functools.partial(kernel, (slots, bs, nsize, count), torus),
        out_shape=(
            jax.ShapeDtypeStruct((2, nsize), f32),
        ),
        in_specs=[
            pl.BlockSpec(memory_space=pl.ANY),
            pl.BlockSpec(memory_space=pl.ANY),
            pl.BlockSpec(memory_space=pl.ANY),
            pl.BlockSpec(memory_space=pl.ANY),
        ],
        out_specs=(pl.BlockSpec(memory_space=vmem),),
        scratch_shapes=[
            pltpu.VMEM((2 * slots, side, side), jnp.bfloat16),
            pltpu.VMEM((side, count), jnp.bfloat16),
            pltpu.VMEM((2, nsize, count), f32),
            pltpu.VMEM((4 * slots, bs, count), f32),
            pltpu.VMEM((4 * slots, bs, count), f32),
            pltpu.VMEM((nsize, count), f32),
            pltpu.VMEM((nz, 1, nsize), f32),
            pltpu.VMEM((nz, nsize), f32),
            pltpu.VMEM((group, nz, nsize), f32),
            pltpu.VMEM((near + 1, piece, count), f32),
            pltpu.VMEM((near, piece, count), f32),
            pltpu.VMEM((near + far, piece, count), f32),
            pltpu.VMEM((piece, count), f32),
            pltpu.VMEM((piece, count), f32),
            pltpu.VMEM((nz, piece, count), f32),
            pltpu.VMEM((group, piece, count), f32),
            pltpu.VMEM((count, nsize), f32),
            pltpu.VMEM((near + 1, nz, nsize), f32),
            pltpu.VMEM((near, nz, nsize), f32),
            pltpu.VMEM((near + far, nz, nsize), f32),
            pltpu.VMEM((nz, 1, nsize), f32),
            pltpu.VMEM((nz, 1, nsize), f32),
            pltpu.VMEM(block_index.shape, jnp.int32),
            pltpu.VMEM((1, count), f32),
            pltpu.SemaphoreType.DMA((phases,)),
            pltpu.SemaphoreType.DMA((phases,)),
            pltpu.SemaphoreType.DMA((slots + 3,)),
        ],
        compiler_params=pltpu.CompilerParams(collective_id=0, has_side_effects=True),
        name="power",
    )(
        block_index,
        shifts.reshape(1, count),
        starts.reshape(1, nsize),
        tensor_blocks.reshape(slots, side, side),
    )
    iterate, estimate = pl.pallas_call(
        tail,
        out_shape=(
            jax.ShapeDtypeStruct((1, nsize), f32),
            jax.ShapeDtypeStruct((1, 1), f32),
        ),
        name="tail",
    )(rows)
    return iterate.reshape(nsize, 1), estimate.reshape(1)


def solution(mesh):
    torus = Mesh(mesh.devices.reshape(TORUS), BLK)
    in_specs = (P(BLK, None, None, None), P(BLK, None), P(None, BLK), P())
    out_specs = (P(None, BLK), P(BLK))
    return jax.shard_map(
        functools.partial(body, TORUS), mesh=torus, in_specs=in_specs, out_specs=out_specs, check_vma=False
    )
```

```python
import functools

import jax
import jax.numpy as jnp
from jax import lax
from jax.experimental import pallas as pl
from jax.experimental.pallas import tpu as pltpu
from jax.sharding import Mesh
from jax.sharding import PartitionSpec as P

BLK = ("y", "z", "x", "c")
TORUS = (4, 8, 4, 2)
MESH = pl.DeviceIdType.MESH
EPS = 1e-06
NEAR = 2


def chip_steps(ny, nx):
    def hops(step):
        return sum(min(s, n - s) for s, n in zip(step, (ny, nx)))

    steps = [(dy, dx) for dy in range(ny) for dx in range(nx)][1:]
    steps.sort(key=lambda step: -hops(step))
    return [d for d in steps if hops(d) > NEAR], [d for d in steps if hops(d) <= NEAR]


def normalized(values):
    return values * lax.rsqrt(jnp.mean(values * values, axis=0, keepdims=True) + EPS)


def slot_weight(idx, blocks_count):
    weight = jnp.where(idx[0] < blocks_count, 6.0, 0.0)
    for other in range(1, 4):
        earlier = jnp.zeros(idx[0].shape, jnp.int32)
        for before in range(other):
            earlier = earlier + jnp.where(idx[before] == idx[other], 1, 0)
        share = jnp.ones(idx[0].shape, jnp.float32)
        for count in range(1, other + 1):
            share = jnp.where(earlier == count, 1.0 / (1 + count), share)
        weight = weight * share
    return weight


def kernel(
    sizes,
    torus,
    bi_hbm,
    shifts_hbm,
    starts_ref,
    tensor_ref,
    out_ref,
    mats,
    pair,
    cur,
    pieces,
    ybuf,
    total,
    zrows,
    ztile,
    cols,
    handed,
    merged,
    arrived,
    zsums,
    zpart,
    zparts,
    image,
    flipped,
    handed2,
    merged2,
    arrived2,
    zsend,
    zlast,
    bi_ref,
    shifts_ref,
    send_sem,
    recv_sem,
    load_sem,
):
    slots, bs, nsize, starts = sizes
    ny, nz, nx, nc = torus
    group = ny * nx * nc
    blocks_count = nsize // bs
    piece = nsize // group
    y, z, x, c = (lax.axis_index(name) for name in BLK)
    me = (y * nx + x) * nc + c

    def at(dy, dx, core):
        py = lax.rem(y + dy, ny)
        px = lax.rem(x + dx, nx)
        return (py, z, px, core), (py * nx + px) * nc + core

    far_steps, near_steps = chip_steps(ny, nx)
    other = 1 - c
    partner, partner_at = at(0, 0, other)
    far = [at(dy, dx, core) for dy, dx in far_steps for core in (c, other)]
    near = [at(dy, dx, c) for dy, dx in near_steps]
    near_other = [at(dy, dx, other) for dy, dx in near_steps]
    plane = far + [peer for pair in zip(near, near_other) for peer in pair]
    plane.append((partner, partner_at))
    line = []
    for dz in sorted(range(1, nz), key=lambda d: -min(d, nz - d)):
        pz = lax.rem(z + dz, nz)
        line.append(((y, pz, x, c), pz))
    everyone = [peer for peer, _ in line + plane]

    barrier = pltpu.get_barrier_semaphore()
    for peer in everyone:
        pl.semaphore_signal(barrier, inc=1, device_id=peer, device_id_type=MESH)
    own = pltpu.make_async_copy(starts_ref, zrows.at[z], load_sem.at[slots])
    own.start()
    small = [
        pltpu.make_async_copy(shifts_hbm, shifts_ref, load_sem.at[slots + 1]),
        pltpu.make_async_copy(bi_hbm, bi_ref, load_sem.at[slots + 2]),
    ]
    for load in small:
        load.start()
    loads = []
    for s in range(slots):
        load = pltpu.make_async_copy(tensor_ref.at[s], mats.at[2 * s], load_sem.at[s])
        load.start()
        loads.append(load)

    own.wait()
    pl.semaphore_wait(barrier, len(everyone))

    def send(phase, src, dst, peer):
        pltpu.make_async_remote_copy(
            src_ref=src,
            dst_ref=dst,
            send_sem=send_sem.at[phase],
            recv_sem=recv_sem.at[phase],
            device_id=peer,
            device_id_type=MESH,
        ).start()

    def wait(sem, span):
        pltpu.make_async_copy(span, span, sem).wait()

    def spread(phase, source, held):
        for peer, _ in plane:
            send(phase, source, held.at[me], peer)

    def spread_done(phase, source, held):
        held[me] = source[...]
        wait(recv_sem.at[phase], held.at[pl.ds(0, group - 1)])

    def collect(phase, source, handed, merged, got):
        rows = got.shape[1]

        def piece_of(place):
            return pl.ds(pl.multiple_of(place * rows, rows), rows)

        for i, (peer, place) in enumerate(far):
            send(phase + 1, source.at[piece_of(place)], got.at[len(near) + i], peer)
        for i, (_, place) in enumerate(near_other):
            send(phase, source.at[piece_of(place)], handed.at[i], partner)
        send(phase, source.at[piece_of(partner_at)], handed.at[len(near)], partner)
        wait(recv_sem.at[phase], handed)
        for i, (peer, place) in enumerate(near):
            merged[i] = source[piece_of(place), :] + handed[i]
            send(phase + 1, merged.at[i], got.at[i], peer)
        return source[piece_of(me), :] + handed[len(near)]

    for peer, _ in line:
        send(0, zrows.at[z], zrows.at[z], peer)

    def flip(s):
        loads[s].wait()
        side = bs * bs
        step = min(side, 256)
        for i in range(0, side, step):
            for j in range(0, side, step):
                tile = mats[2 * s, i : i + step, j : j + step]
                mats[2 * s + 1, j : j + step, i : i + step] = tile.T

    wait(recv_sem.at[0], zrows.at[pl.ds(0, nz - 1)])
    ztile[...] = zrows[...].reshape(nz, nsize)
    spread(1, ztile, cols)
    for load in small:
        load.wait()
    column = ((y * nz + z) * nx + x) * nc + c
    lane = lax.broadcasted_iota(jnp.int32, (1, starts), 1)
    own_shift = jnp.sum(jnp.where(lane == column, shifts_ref[...], 0.0), axis=1, keepdims=True)
    held = lax.broadcasted_iota(jnp.int32, (starts, starts), 1)
    given = lax.broadcasted_iota(jnp.int32, (starts, starts), 0)
    hz = held % nz
    hc = (held // nz) % nc
    hx = (held // (nz * nc)) % nx
    hy = held // (nz * nc * nx)
    where_from = ((hy * nz + hz) * nx + hx) * nc + hc
    chosen = jnp.where(given == where_from, 1.0, 0.0).astype(jnp.float32)
    shifts = jnp.dot(
        jnp.broadcast_to(shifts_ref[...], (8, starts)),
        chosen,
        precision=lax.Precision.HIGHEST,
        preferred_element_type=jnp.float32,
    )[0:1, :]

    for s in range(slots):
        flip(s)
    spread_done(1, ztile, cols)
    cur[0] = normalized(cols[...].reshape(starts, nsize).T)

    def index(s, position):
        return bi_ref[s : s + 1, position : position + 1]

    def spot(s, position):
        safe = jnp.minimum(index(s, position), blocks_count - 1)
        return jnp.broadcast_to(safe, (bs, starts))

    def contract(turn):
        for s in range(slots):
            for position in range(4):
                at = spot(s, position)
                rows = cur[turn, 0:bs, :]
                for p in range(1, blocks_count):
                    rows = jnp.where(at == p, cur[turn, p * bs : (p + 1) * bs, :], rows)
                pieces[4 * s + position] = rows

        def one(q, carry):
            s = q // 2
            m = q % 2
            side = bs * bs

            def rows(position):
                return pieces[4 * s + position]

            first, second = rows(2 - 2 * m), rows(3 - 2 * m)
            for a in range(bs):
                pair[a * bs : (a + 1) * bs, :] = (first[a : a + 1, :] * second).astype(
                    jnp.bfloat16
                )
            lead, trail = rows(2 * m), rows(2 * m + 1)
            down = jnp.zeros((bs, starts), jnp.float32)
            per = min(bs, 8)
            for t in range(0, bs, per):
                part = jnp.dot(
                    mats[q, t * bs : (t + per) * bs, :],
                    pair[...],
                    preferred_element_type=jnp.float32,
                ).reshape(per, bs, starts)
                ybuf[2 * q, t : t + per, :] = jnp.sum(part * trail[None], axis=1)
                for a in range(per):
                    down = down + part[a] * lead[t + a : t + a + 1, :]
            ybuf[2 * q + 1] = down
            return carry

        lax.fori_loop(0, 2 * slots, one, 0, unroll=True)
        sums = [jnp.zeros((bs, starts), jnp.float32) for _ in range(blocks_count)]
        for s in range(slots):
            weight = slot_weight([index(s, position) for position in range(4)], blocks_count)
            for position in range(4):
                part = ybuf[4 * s + position] * weight
                at = spot(s, position)
                for p in range(blocks_count):
                    sums[p] = sums[p] + jnp.where(at == p, part, 0.0)
        return sums

    sums = contract(0)
    for p in range(blocks_count):
        total[p * bs : (p + 1) * bs, :] = sums[p]
    own_piece = collect(4, total, handed, merged, arrived)
    wait(recv_sem.at[5], arrived)
    zpart[...] = own_piece + jnp.sum(arrived[...], axis=0)
    for peer, _ in line:
        send(6, zpart, zparts.at[z], peer)
    zparts[z] = zpart[...]
    wait(recv_sem.at[6], zparts.at[pl.ds(0, nz - 1)])
    zsums[...] = jnp.sum(zparts[...], axis=0)
    spread(7, zsums, image)
    spread_done(7, zsums, image)
    cur[1] = normalized(image[...].reshape(nsize, starts) + shifts * cur[0])

    sums = contract(1)
    for p in range(blocks_count):
        flipped[:, p * bs : (p + 1) * bs] = sums[p].T
    own_piece = collect(10, flipped, handed2, merged2, arrived2)
    cols[...] = cur[1].T.reshape(group, nz, nsize)
    wait(recv_sem.at[11], arrived2)
    zsend[...] = (own_piece + jnp.sum(arrived2[...], axis=0)).reshape(nz, 1, nsize)
    for peer, place in line:
        send(12, zsend.at[place], zlast.at[z], peer)
    zlast[z] = zsend[z]
    previous = cols[me, pl.ds(z, 1), :]
    wait(recv_sem.at[12], zlast.at[pl.ds(0, nz - 1)])
    mine = jnp.sum(zlast[...], axis=0)
    last = mine + own_shift * previous
    out_ref[0:1, :] = last * lax.rsqrt(jnp.mean(last * last, axis=1, keepdims=True) + EPS)
    scale = lax.rsqrt(jnp.mean(mine * mine, axis=1, keepdims=True) + EPS)
    out_ref[1:2, :] = previous * mine * (scale / nsize)

    sent = [(0, zrows, nz - 1), (6, zparts, nz - 1), (12, zlast, nz - 1)]
    for phase, span in ((1, cols), (7, image)):
        sent.append((phase, span, group - 1))
    for phase, span, span2 in ((4, handed, arrived), (10, handed2, arrived2)):
        sent += [(phase, span, len(near) + 1), (phase + 1, span2, len(near) + len(far))]
    for phase, span, count in sent:
        if count:
            wait(send_sem.at[phase], span.at[pl.ds(0, count)])


def tail(rows_ref, out_ref, est_ref):
    out_ref[...] = rows_ref[0:1, :]
    est_ref[...] = jnp.sum(rows_ref[1:2, :], axis=1, keepdims=True)


def body(torus, tensor_blocks, block_index, starts, shifts):
    slots, bs = tensor_blocks.shape[:2]
    nsize = starts.shape[0]
    count = shifts.shape[0]
    ny, nz, nx, nc = torus
    group = ny * nx * nc
    piece = nsize // group
    side = bs * bs
    f32 = jnp.float32
    vmem = pltpu.MemorySpace.VMEM
    far, near = (len(part) for part in chip_steps(ny, nx))
    far = far * nc
    phases = 13
    (rows,) = pl.pallas_call(
        functools.partial(kernel, (slots, bs, nsize, count), torus),
        out_shape=(
            jax.ShapeDtypeStruct((2, nsize), f32),
        ),
        in_specs=[
            pl.BlockSpec(memory_space=pl.ANY),
            pl.BlockSpec(memory_space=pl.ANY),
            pl.BlockSpec(memory_space=pl.ANY),
            pl.BlockSpec(memory_space=pl.ANY),
        ],
        out_specs=(pl.BlockSpec(memory_space=vmem),),
        scratch_shapes=[
            pltpu.VMEM((2 * slots, side, side), jnp.bfloat16),
            pltpu.VMEM((side, count), jnp.bfloat16),
            pltpu.VMEM((2, nsize, count), f32),
            pltpu.VMEM((4 * slots, bs, count), f32),
            pltpu.VMEM((4 * slots, bs, count), f32),
            pltpu.VMEM((nsize, count), f32),
            pltpu.VMEM((nz, 1, nsize), f32),
            pltpu.VMEM((nz, nsize), f32),
            pltpu.VMEM((group, nz, nsize), f32),
            pltpu.VMEM((near + 1, piece, count), f32),
            pltpu.VMEM((near, piece, count), f32),
            pltpu.VMEM((near + far, piece, count), f32),
            pltpu.VMEM((piece, count), f32),
            pltpu.VMEM((piece, count), f32),
            pltpu.VMEM((nz, piece, count), f32),
            pltpu.VMEM((group, piece, count), f32),
            pltpu.VMEM((count, nsize), f32),
            pltpu.VMEM((near + 1, nz, nsize), f32),
            pltpu.VMEM((near, nz, nsize), f32),
            pltpu.VMEM((near + far, nz, nsize), f32),
            pltpu.VMEM((nz, 1, nsize), f32),
            pltpu.VMEM((nz, 1, nsize), f32),
            pltpu.VMEM(block_index.shape, jnp.int32),
            pltpu.VMEM((1, count), f32),
            pltpu.SemaphoreType.DMA((phases,)),
            pltpu.SemaphoreType.DMA((phases,)),
            pltpu.SemaphoreType.DMA((slots + 3,)),
        ],
        compiler_params=pltpu.CompilerParams(collective_id=0, has_side_effects=True, vmem_limit_bytes=63963136),
        name="power",
    )(
        block_index,
        shifts.reshape(1, count),
        starts.reshape(1, nsize),
        tensor_blocks.reshape(slots, side, side),
    )
    iterate, estimate = pl.pallas_call(
        tail,
        out_shape=(
            jax.ShapeDtypeStruct((1, nsize), f32),
            jax.ShapeDtypeStruct((1, 1), f32),
        ),
        compiler_params=pltpu.CompilerParams(vmem_limit_bytes=1024 * 1024),
        name="tail",
    )(rows)
    return iterate.reshape(nsize, 1), estimate.reshape(1)


def solution(mesh):
    torus = Mesh(mesh.devices.reshape(TORUS), BLK)
    in_specs = (P(BLK, None, None, None), P(BLK, None), P(None, BLK), P())
    out_specs = (P(None, BLK), P(BLK))
    return jax.shard_map(
        functools.partial(body, TORUS), mesh=torus, in_specs=in_specs, out_specs=out_specs, check_vma=False
    )
```
